32 devices in a mesh: groups: 1, ep: 32 (over z, y, x, core).
Axes of the slice: x: 2, y: 2, z: 4, core: 2. Of those that a mesh axis runs over, the one named last changes fastest.
Arguments:
- tokens: bfloat16 [256, 7168], P(('groups', 'ep')), may hold values from -6 to 6
- expert_ids: int32 [256, 2], P(('groups', 'ep')), may hold values from 0 to 3, all different within a row; in each aligned block of 8 rows (0 to 7, 8 to 15, ...) at most 8 rows name the same one
- affinity: float32 [256, 2], P(('groups', 'ep')), may hold values from 0.05 to 1
- w_gate: bfloat16 [32, 7168, 256], P('ep'), may hold values from -0.0625 to 0.0625
- w_up: bfloat16 [32, 7168, 256], P('ep'), may hold values from -0.0625 to 0.0625
- w_down: bfloat16 [32, 256, 7168], P('ep'), may hold values from -0.125 to 0.125
Outputs:
- moe_out: bfloat16 [256, 7168], P(('groups', 'ep'))
The draws below stay inside these ranges and needn't reach their ends.
Inputs may be any that keep to these rules, and one draw needn't show every extreme that they name: `expert_ids`: each token names 2 different experts. Among the 8 tokens of one device no expert is named more than 8 times, and in every draw some device names some expert exactly 8 times.
All inputs are finite; a program needn't handle non-finite values.
Results may differ from the reference program's by a relative error of at most 0.008.
Values may be sent and summed in bfloat16 or wider, within the bound.
A program may use at most 128 MiB of HBM per device.

```python
import math
import jax
import jax.numpy as jnp
import numpy as np
from jax import lax

D = 7168
FF = 2048
SPLIT = 8
ROUTES = 2
TOK_DEV = 8
HID_DEV = 256
EXPERTS = 4
PIECES = 32
CAP = 8
TOKENS = 256
N_EP = 32


def block_levels(rng, dims, cuts, smallest, top_value):
    level = 1.0
    for axis_at, parts in cuts:
        heights = jax.random.uniform(jax.random.fold_in(jax.random.fold_in(rng, 6), axis_at), (parts,), jnp.float32, smallest / len(cuts), top_value / len(cuts))
        level = level * jnp.repeat(jnp.exp(heights), dims[axis_at] // parts).reshape((-1,) + (1,) * (len(dims) - 1 - axis_at))
    return level


def assign_block(own_key, own, number, rows, count, top, most, skew):
    order = jax.random.permutation(own_key, count)
    heavy_load, usual = portions_of(count, rows * top, most, skew, True), portions_of(count, rows * top, most, skew, False)
    places = jnp.arange(count)

    def named(sizes, turn):
        used = int((sizes > 0).sum())
        fixed = max(1, used // 4)
        shifted = fixed + (places - fixed + turn * (used - fixed)) % max(1, count - fixed)
        return jnp.zeros((count,), jnp.int32).at[order[jnp.where(places < fixed, places, shifted)]].set(jnp.asarray(sizes, jnp.int32))

    sizes = jnp.where(number % 4 == 0, named(heavy_load, number // 4), named(usual, number - number // 4 - 1))
    mixed = jax.random.permutation(jax.random.fold_in(own, 3), count)
    donor, taker = mixed[0:count // 2 * 2:2], mixed[1:count // 2 * 2:2]
    margin = jnp.minimum(sizes[donor] - 1, most - sizes[taker]) // 2
    margin = jnp.where((donor == order[0]) | (taker == order[0]) | (sizes[taker] == 0), 0, jnp.maximum(margin, 0))
    shifted = jax.random.randint(jax.random.fold_in(own, 4), (count // 2,), 0, 1 << 20) % (margin + 1)
    sizes = sizes.at[donor].add(-shifted).at[taker].add(shifted)
    labels = jnp.searchsorted(jnp.cumsum(sizes), jnp.arange(rows * top), side="right").astype(jnp.int32)
    listing = labels.reshape(top, rows).T
    listing = listing[jax.random.permutation(jax.random.fold_in(own, 1), rows)]
    turn = jax.random.randint(jax.random.fold_in(own, 2), (rows, 1), 0, top)
    return jnp.take_along_axis(listing, (jnp.arange(top)[None, :] + turn) % top, axis=1)


def portions_of(number_of, total, limit, lean, full):
    portions = [(1 << 20) // math.isqrt(standing ** lean) + 1 for standing in range(1, number_of + 1)]
    largest = limit if full else min(limit, max(-(-total // number_of), total * portions[0] // sum(portions)))
    least = 1 if total - largest >= number_of - 1 else 0
    given, spare = [largest] + [least] * (number_of - 1), total - largest - least * (number_of - 1)
    while spare > 0:
        candidates = [i for i in range(1, number_of) if given[i] < largest] or [i for i in range(1, number_of) if given[i] < limit]
        whole, budget = sum([portions[i] for i in candidates]), spare
        for i in candidates:
            more = min(limit - given[i], max(1, budget * portions[i] // whole), spare)
            given[i] = given[i] + more
            spare = spare - more
    return np.array(given)


def scatter_about(stream_key, shape, width, bound, shards=(), kind=jnp.bfloat16):
    factor_of = block_levels(stream_key, shape, shards, -0.22, 0.18) if shards else 1.0
    drawn = jax.random.normal(stream_key, shape, jnp.float32) * width * factor_of
    return jnp.minimum(jnp.maximum(drawn, -bound), bound).astype(kind)


def setup_inputs(seed: int = 0, part: int = 0) -> dict:
    keys = jax.random.split(jax.random.key(seed), 7)
    part_keys = jax.random.split(jax.random.fold_in(keys[6], part), 7)
    tokens = scatter_about(part_keys[0], (TOKENS, D), 1.0, 6.0, ((0, 32),))
    expert_ids_keys = jax.random.split(jax.random.fold_in(part_keys[1], 1), TOKENS // TOK_DEV)
    expert_ids_turns = jax.random.permutation(jax.random.fold_in(part_keys[1], 3), TOKENS // TOK_DEV)
    expert_ids = jax.vmap(lambda own, number: assign_block(jax.random.fold_in(part_keys[1], 2), own, number, TOK_DEV, EXPERTS, ROUTES, CAP, 2))(expert_ids_keys, expert_ids_turns).reshape((TOKENS, ROUTES))
    affinity = jnp.clip(jnp.exp(math.log(1.0) - 2.9957323 * jax.random.uniform(part_keys[2], (TOKENS, ROUTES), jnp.float32) ** block_levels(part_keys[2], (TOKENS, ROUTES), ((0, 32),), -0.2, 0.2)), 0.05, 1.0)
    w_gate = scatter_about(keys[3], (PIECES, D, HID_DEV), D ** -0.5, 0.0625, ((0, 32),))
    w_up = scatter_about(keys[4], (PIECES, D, HID_DEV), D ** -0.5, 0.0625, ((0, 32),))
    w_down = scatter_about(keys[5], (PIECES, HID_DEV, D), FF ** -0.5, 0.125, ((0, 32),))
    return {"tokens": tokens, "expert_ids": expert_ids, "affinity": affinity, "w_gate": w_gate, "w_up": w_up, "w_down": w_down}


route_scale = 2.5


def reference(tokens, expert_ids, affinity, w_gate, w_up, w_down):
    route_weight = route_scale * affinity / jnp.sum(affinity, axis=1, keepdims=True)
    onehot = (expert_ids.reshape(N_EP, TOK_DEV * ROUTES, 1) == jnp.arange(EXPERTS, dtype=jnp.int32)[None, None, :]).astype(jnp.int32)
    earlier = jnp.cumsum(onehot, axis=1) - onehot
    slot = jnp.sum(earlier * onehot, axis=2).reshape(TOKENS, ROUTES).astype(jnp.int32)
    source = (jnp.arange(TOKENS, dtype=jnp.int32) // TOK_DEV)[:, None]
    position = (source * CAP + slot).astype(jnp.int32)
    token_index = jnp.broadcast_to(jnp.arange(TOKENS, dtype=jnp.int32)[:, None], (TOKENS, ROUTES))
    table = jnp.full((EXPERTS, N_EP * CAP), TOKENS, jnp.int32).at[expert_ids, position].set(token_index)
    padded = jnp.concatenate([tokens, jnp.zeros((1, D), jnp.bfloat16)], axis=0)

    def expert_rows(expert):
        rows = padded[table[expert]]
        total = jnp.zeros((N_EP * CAP, D), jnp.float32)
        for piece_slot in range(SPLIT):
            piece = (expert * SPLIT + piece_slot).astype(jnp.int32)
            gate_piece = lax.dynamic_index_in_dim(w_gate, piece, 0, keepdims=False)
            up_piece = lax.dynamic_index_in_dim(w_up, piece, 0, keepdims=False)
            down_piece = lax.dynamic_index_in_dim(w_down, piece, 0, keepdims=False)
            gate = jnp.dot(rows, gate_piece, preferred_element_type=jnp.float32)
            up = jnp.dot(rows, up_piece, preferred_element_type=jnp.float32)
            hidden = (jax.nn.silu(gate) * up).astype(jnp.bfloat16)
            partial_value = jnp.dot(hidden, down_piece, preferred_element_type=jnp.float32).astype(jnp.bfloat16)
            total = total + partial_value.astype(jnp.float32)
        return total

    outputs = lax.map(expert_rows, jnp.arange(EXPERTS, dtype=jnp.int32))
    picked = outputs[expert_ids, position]
    return jnp.sum(route_weight[:, :, None] * picked, axis=1).astype(jnp.bfloat16)
```

```python
import functools

import jax
import jax.numpy as jnp
from jax import lax
from jax.experimental import pallas as pl
from jax.experimental.pallas import tpu as pltpu
from jax.sharding import PartitionSpec as P

SPLIT = 8
CORES = 2
QUADS = SPLIT // CORES
MESH = pl.DeviceIdType.MESH
VMEM_LIMIT = 63 * 1024 * 1024

route_scale = 2.5


def tile_of(size, most):
    best = 128
    for tile in range(128, most + 1, 128):
        if size % tile == 0:
            best = tile
    return best


def kernel(
    experts,
    tok_hbm, ids_ref, aff_ref, gate_hbm, up_hbm, down_hbm,
    out_ref,
    tok, part, rb3, rb2, rb1, rb0, gate_w, up_w, down_w,
    load_sem, w_sem, tok_recv, z_send, s1_send, s2_send, s3_send,
    r3_recv, r3_send, r2_recv, r2_send, r1_recv, r1_send, r0_recv, r0_send,
):
    E = experts
    rows, width = tok_hbm.shape
    hid = gate_w.shape[1]
    me = lax.axis_index("ep")
    z = me // SPLIT
    j = me % SPLIT
    c = j % 2
    x = (j // 2) % 2
    y = j // 4
    dx = 2 * (1 - 2 * x)
    dy = 4 * (1 - 2 * y)
    ja = j + (1 - c) * dy + c * dx
    jb = j + c * dy + (1 - c) * dx
    jab = j + dx + dy
    js = j + 1 - 2 * c
    base = z * SPLIT
    dev_a, dev_b, dev_s = base + ja, base + jb, base + js

    def plane(k):
        return (z + k) % E

    loads = [
        pltpu.make_async_copy(tok_hbm, tok.at[me], load_sem),
        pltpu.make_async_copy(gate_hbm.at[0], gate_w, w_sem.at[0]),
        pltpu.make_async_copy(up_hbm.at[0], up_w, w_sem.at[1]),
        pltpu.make_async_copy(down_hbm.at[0], down_w, w_sem.at[2]),
    ]
    for load in loads:
        load.start()

    barrier = pltpu.get_barrier_semaphore()
    peers = [dev_a, dev_b, dev_s] + [((z + k) % E) * SPLIT + j for k in range(1, E)]
    for peer in peers:
        pl.semaphore_signal(barrier, inc=1, device_id={"ep": peer}, device_id_type=MESH)
    pl.semaphore_wait(barrier, len(peers))

    sends = []

    def send(src, dst, send_sem, recv_sem, device):
        copy = pltpu.make_async_remote_copy(
            src_ref=src, dst_ref=dst, send_sem=send_sem, recv_sem=recv_sem,
            device_id={"ep": device}, device_id_type=MESH,
        )
        copy.start()
        sends.append(copy)

    def arrived(dst, recv_sem):
        pltpu.make_async_remote_copy(
            src_ref=dst, dst_ref=dst, send_sem=load_sem, recv_sem=recv_sem,
            device_id={"ep": dev_s}, device_id_type=MESH,
        ).wait_recv()

    def tok_arrived(unit):
        arrived(tok.at[unit], tok_recv.at[unit])

    def pass_on(src, unit, sem, device):
        send(src, tok.at[unit], sem, tok_recv.at[unit], device)

    def own(k):
        return tok_hbm if k == 0 else tok.at[plane(k) * SPLIT + j]

    def f1(k):
        unit = plane(k) * SPLIT + j
        if k > 0:
            tok_arrived(unit)
        pass_on(own(k), unit, s1_send.at[k], dev_a)
        pass_on(own(k), unit, s3_send.at[k, 0], dev_s)

    def f2(k):
        unit, unit_a = plane(k) * SPLIT + j, plane(k) * SPLIT + ja
        pass_on(own(k), unit, s2_send.at[k, 0], dev_b)
        tok_arrived(unit_a)
        pass_on(tok.at[unit_a], unit_a, s2_send.at[k, 1], dev_b)
        pass_on(tok.at[unit_a], unit_a, s3_send.at[k, 1], dev_s)

    def f3(k):
        for at, jj in ((2, jb), (3, jab)):
            unit = plane(k) * SPLIT + jj
            tok_arrived(unit)
            pass_on(tok.at[unit], unit, s3_send.at[k, at], dev_s)

    k_tile = tile_of(width, 1792)
    n_tile = tile_of(width, 1024)

    def compute(k):
        first = plane(k) * SPLIT
        if k == 0:
            for load in loads:
                load.wait()
        for q in range(QUADS):
            tok_arrived(first + 2 * q + (1 - c))

        def up_step(t, acc):
            cols = pl.ds(pl.multiple_of(t * k_tile, k_tile), k_tile)
            xs = tok[pl.ds(first, SPLIT), :, cols]
            xs = xs.astype(jnp.float32).reshape(SPLIT * rows, k_tile).astype(jnp.bfloat16)
            g, u = acc
            g = g + jnp.dot(xs, gate_w[cols, :], preferred_element_type=jnp.float32)
            u = u + jnp.dot(xs, up_w[cols, :], preferred_element_type=jnp.float32)
            return g, u

        zero = jnp.zeros((SPLIT * rows, hid), jnp.float32)
        g, u = lax.fori_loop(0, width // k_tile, up_step, (zero, zero))
        hidden = (jax.nn.silu(g) * u).astype(jnp.bfloat16)

        def down_step(t, carry):
            cols = pl.ds(pl.multiple_of(t * n_tile, n_tile), n_tile)
            d = jnp.dot(hidden, down_w[:, cols], preferred_element_type=jnp.float32)
            part[pl.ds(first, SPLIT), :, cols] = d.reshape(SPLIT, rows, n_tile).astype(jnp.bfloat16)
            return carry

        lax.fori_loop(0, width // n_tile, down_step, 0)
        for q in range(QUADS):
            send(part.at[first + 2 * q + (1 - c)], rb3.at[k, q],
                 r3_send.at[k, q], r3_recv.at[k, q], dev_s)

    f32 = jnp.float32

    def r2(k):
        for at, jj in ((1, jab), (0, jb)):
            unit, q = plane(k) * SPLIT + jj, jj // 2
            arrived(rb3.at[k, q], r3_recv.at[k, q])
            part[unit] = (part[unit].astype(f32) + rb3[k, q].astype(f32)).astype(jnp.bfloat16)
            send(part.at[unit], rb2.at[k, at], r2_send.at[k, at], r2_recv.at[k, at], dev_b)

    def r1(k):
        unit, q = plane(k) * SPLIT + ja, ja // 2
        arrived(rb3.at[k, q], r3_recv.at[k, q])
        arrived(rb2.at[k, 1], r2_recv.at[k, 1])
        part[unit] = (
            part[unit].astype(f32) + rb3[k, q].astype(f32) + rb2[k, 1].astype(f32)
        ).astype(jnp.bfloat16)
        send(part.at[unit], rb1.at[k], r1_send.at[k], r1_recv.at[k], dev_a)

    def r0(k):
        unit, q = plane(k) * SPLIT + j, j // 2
        arrived(rb3.at[k, q], r3_recv.at[k, q])
        arrived(rb2.at[k, 0], r2_recv.at[k, 0])
        arrived(rb1.at[k], r1_recv.at[k])
        part[unit] = (
            (part[unit].astype(f32) + rb3[k, q].astype(f32))
            + (rb2[k, 0].astype(f32) + rb1[k].astype(f32))
        ).astype(jnp.bfloat16)
        if k > 0:
            send(part.at[unit], rb0.at[k], r0_send.at[k], r0_recv.at[k], unit)

    for k in range(1, E):
        pass_on(tok_hbm, me, z_send.at[k], ((z + E - k) % E) * SPLIT + j)
    f1(0)
    for i in range(E + 3):
        steps = ((f2, i), (f1, i + 1), (r2, i - 2), (compute, i - 1), (f3, i), (r1, i - 2), (r0, i - 3))
        for step, k in steps:
            if 0 <= k < E:
                step(k)

    affinity = aff_ref[...]
    weight = route_scale * affinity / jnp.sum(affinity, axis=1, keepdims=True)
    ids = ids_ref[...]

    def weighted(values, expert):
        w = jnp.sum(jnp.where(ids == expert, weight, 0.0), axis=1, keepdims=True)
        return w * values.astype(f32)

    total = weighted(part[me], z)
    for k in range(1, E):
        arrived(rb0.at[k], r0_recv.at[k])
        total = total + weighted(rb0[k], (z + E - k) % E)
    out_ref[...] = total.astype(out_ref.dtype)
    for copy in sends:
        copy.wait_send()


def body(tokens, expert_ids, affinity, w_gate, w_up, w_down):
    n = lax.axis_size("ep")
    experts = n // SPLIT
    rows, width = tokens.shape
    hid = w_gate.shape[2]
    dma = pltpu.SemaphoreType.DMA
    bf16 = jnp.bfloat16
    unit = (rows, width)
    hbm = pl.BlockSpec(memory_space=pltpu.MemorySpace.HBM)
    vmem = pl.BlockSpec(memory_space=pltpu.MemorySpace.VMEM)
    return pl.pallas_call(
        functools.partial(kernel, experts),
        out_shape=jax.ShapeDtypeStruct(unit, bf16),
        in_specs=[hbm, vmem, vmem, hbm, hbm, hbm],
        out_specs=vmem,
        scratch_shapes=[
            pltpu.VMEM((n,) + unit, bf16),
            pltpu.VMEM((n,) + unit, bf16),
            pltpu.VMEM((experts, QUADS) + unit, bf16),
            pltpu.VMEM((experts, 2) + unit, bf16),
            pltpu.VMEM((experts,) + unit, bf16),
            pltpu.VMEM((experts,) + unit, bf16),
            pltpu.VMEM((width, hid), bf16),
            pltpu.VMEM((width, hid), bf16),
            pltpu.VMEM((hid, width), bf16),
            dma,
            dma((3,)),
            dma((n,)),
            dma((experts,)),
            dma((experts,)),
            dma((experts, 2)),
            dma((experts, QUADS)),
            dma((experts, QUADS)),
            dma((experts, QUADS)),
            dma((experts, 2)),
            dma((experts, 2)),
            dma((experts,)),
            dma((experts,)),
            dma((experts,)),
            dma((experts,)),
        ],
        compiler_params=pltpu.CompilerParams(
            collective_id=0, has_side_effects=True, vmem_limit_bytes=VMEM_LIMIT
        ),
    )(tokens, expert_ids, affinity, w_gate, w_up, w_down)


def solution(mesh):
    return jax.shard_map(
        body,
        mesh=mesh,
        in_specs=(
            P(("groups", "ep"), None),
            P(("groups", "ep"), None),
            P(("groups", "ep"), None),
            P("ep", None, None),
            P("ep", None, None),
            P("ep", None, None),
        ),
        out_specs=P(("groups", "ep"), None),
        check_vma=False,
    )
```

```python
import functools

import jax
import jax.numpy as jnp
from jax import lax
from jax.experimental import pallas as pl
from jax.experimental.pallas import tpu as pltpu
from jax.sharding import PartitionSpec as P

SPLIT = 8
CORES = 2
QUADS = SPLIT // CORES
MESH = pl.DeviceIdType.MESH
VMEM_LIMIT = 63 * 1024 * 1024

route_scale = 2.5


def tile_of(size, most):
    best = 128
    for tile in range(128, most + 1, 128):
        if size % tile == 0:
            best = tile
    return best


def shifts(experts):
    shift = [0]
    for step in range(1, experts // 2 + 1):
        shift += [step] if 2 * step == experts else [step, experts - step]
    return shift


def kernel(
    experts,
    tok_hbm, gate_hbm, up_hbm, down_hbm,
    out_ref,
    tok, part, rb3, rb2, rb1, rb0, gate_w, up_w, down_w,
    load_sem, w_sem, tok_recv, z_send, s1_send, s2_send, s3_send,
    r3_recv, r3_send, r2_recv, r2_send, r1_recv, r1_send, r0_recv, r0_send,
):
    E = experts
    rows, width = tok_hbm.shape
    hid = gate_w.shape[1]
    me = lax.axis_index("ep")
    z = me // SPLIT
    j = me % SPLIT
    c = j % 2
    x = (j // 2) % 2
    y = j // 4
    dx = 2 * (1 - 2 * x)
    dy = 4 * (1 - 2 * y)
    ja = j + (1 - c) * dy + c * dx
    jb = j + c * dy + (1 - c) * dx
    jab = j + dx + dy
    js = j + 1 - 2 * c
    base = z * SPLIT
    dev_a, dev_b, dev_s = base + ja, base + jb, base + js

    shift = shifts(E)

    def plane(k):
        return (z + shift[k]) % E

    def plane_back(k):
        return (z + E - shift[k]) % E

    loads = [
        pltpu.make_async_copy(tok_hbm, tok.at[me], load_sem),
        pltpu.make_async_copy(gate_hbm.at[0], gate_w, w_sem.at[0]),
        pltpu.make_async_copy(up_hbm.at[0], up_w, w_sem.at[1]),
        pltpu.make_async_copy(down_hbm.at[0], down_w, w_sem.at[2]),
    ]
    for load in loads:
        load.start()

    barrier = pltpu.get_barrier_semaphore()
    peers = [dev_a, dev_b, dev_s] + [((z + k) % E) * SPLIT + j for k in range(1, E)]
    for peer in peers:
        pl.semaphore_signal(barrier, inc=1, device_id={"ep": peer}, device_id_type=MESH)
    pl.semaphore_wait(barrier, len(peers))

    sends = []

    def send(src, dst, send_sem, recv_sem, device):
        copy = pltpu.make_async_remote_copy(
            src_ref=src, dst_ref=dst, send_sem=send_sem, recv_sem=recv_sem,
            device_id={"ep": device}, device_id_type=MESH,
        )
        copy.start()
        sends.append(copy)

    def arrived(dst, recv_sem):
        pltpu.make_async_remote_copy(
            src_ref=dst, dst_ref=dst, send_sem=load_sem, recv_sem=recv_sem,
            device_id={"ep": dev_s}, device_id_type=MESH,
        ).wait_recv()

    def tok_arrived(unit):
        arrived(tok.at[unit], tok_recv.at[unit])

    def pass_on(src, unit, sem, device):
        send(src, tok.at[unit], sem, tok_recv.at[unit], device)

    def own(k):
        return tok_hbm if k == 0 else tok.at[plane(k) * SPLIT + j]

    def f1(k):
        unit = plane(k) * SPLIT + j
        if k > 0:
            tok_arrived(unit)
        pass_on(own(k), unit, s1_send.at[k], dev_a)
        pass_on(own(k), unit, s2_send.at[k, 0], dev_b)
        pass_on(own(k), unit, s3_send.at[k, 0], dev_s)

    def f2(k):
        unit_a = plane(k) * SPLIT + ja
        tok_arrived(unit_a)
        pass_on(tok.at[unit_a], unit_a, s2_send.at[k, 1], dev_b)
        pass_on(tok.at[unit_a], unit_a, s3_send.at[k, 1], dev_s)

    def f3(k, at=2, jj=jb):
        unit = plane(k) * SPLIT + jj
        tok_arrived(unit)
        pass_on(tok.at[unit], unit, s3_send.at[k, at], dev_s)

    def f4(k):
        f3(k, 3, jab)

    k_tile = tile_of(width, 1792)
    n_tile = tile_of(width, 1024)

    held = {}

    def up(k, half):
        first = plane(k) * SPLIT
        if k == 0 and half == 0:
            for load in loads:
                load.wait()
        if half == 0:
            for q in range(QUADS):
                tok_arrived(first + 2 * q + (1 - c))

        def up_step(t, acc):
            cols = pl.ds(pl.multiple_of(t * k_tile, k_tile), k_tile)
            xs = tok[pl.ds(first, SPLIT), :, cols]
            xs = xs.astype(jnp.float32).reshape(SPLIT * rows, k_tile).astype(jnp.bfloat16)
            g, u = acc
            g = g + jnp.dot(xs, gate_w[cols, :], preferred_element_type=jnp.float32)
            u = u + jnp.dot(xs, up_w[cols, :], preferred_element_type=jnp.float32)
            return g, u

        zero = jnp.zeros((SPLIT * rows, hid), jnp.float32)
        count = width // k_tile
        if half == 0:
            held[k] = lax.fori_loop(0, count // 2, up_step, (zero, zero))
        else:
            g, u = lax.fori_loop(count // 2, count, up_step, held[k])
            held[k] = (jax.nn.silu(g) * u).astype(jnp.bfloat16)

    def down(k):
        first = plane(k) * SPLIT
        hidden = held.pop(k)

        def down_step(t, carry):
            cols = pl.ds(pl.multiple_of(t * n_tile, n_tile), n_tile)
            d = jnp.dot(hidden, down_w[:, cols], preferred_element_type=jnp.float32)
            part[pl.ds(first, SPLIT), :, cols] = d.reshape(SPLIT, rows, n_tile).astype(jnp.bfloat16)
            return carry

        lax.fori_loop(0, width // n_tile, down_step, 0)
        for q in range(QUADS):
            send(part.at[first + 2 * q + (1 - c)], rb3.at[k, q],
                 r3_send.at[k, q], r3_recv.at[k, q], dev_s)

    f32 = jnp.float32

    def ra(k, at=1, jj=jab):
        unit, q = plane(k) * SPLIT + jj, jj // 2
        arrived(rb3.at[k, q], r3_recv.at[k, q])
        part[unit] = (part[unit].astype(f32) + rb3[k, q].astype(f32)).astype(jnp.bfloat16)
        send(part.at[unit], rb2.at[k, at], r2_send.at[k, at], r2_recv.at[k, at], dev_b)

    def rb(k):
        ra(k, 0, jb)

    def r1(k):
        unit, q = plane(k) * SPLIT + ja, ja // 2
        arrived(rb3.at[k, q], r3_recv.at[k, q])
        arrived(rb2.at[k, 1], r2_recv.at[k, 1])
        part[unit] = (
            part[unit].astype(f32) + rb3[k, q].astype(f32) + rb2[k, 1].astype(f32)
        ).astype(jnp.bfloat16)
        send(part.at[unit], rb1.at[k], r1_send.at[k], r1_recv.at[k], dev_a)

    def r0(k):
        unit, q = plane(k) * SPLIT + j, j // 2
        arrived(rb3.at[k, q], r3_recv.at[k, q])
        arrived(rb2.at[k, 0], r2_recv.at[k, 0])
        arrived(rb1.at[k], r1_recv.at[k])
        part[unit] = (
            (part[unit].astype(f32) + rb3[k, q].astype(f32))
            + (rb2[k, 0].astype(f32) + rb1[k].astype(f32))
        ).astype(jnp.bfloat16)
        if k > 0:
            send(part.at[unit], rb0.at[k], r0_send.at[k], r0_recv.at[k], unit)

    for k in range(1, E):
        pass_on(tok_hbm, me, z_send.at[k], plane_back(k) * SPLIT + j)
    steps = {
        "f1": f1, "f2": f2, "f3": f3, "f4": f4,
        "up0": lambda k: up(k, 0), "up1": lambda k: up(k, 1), "down": down,
        "ra": ra, "rb": rb, "r1": r1, "r0": r0,
    }
    for i in range(-1, E + 5):
        for name, k in (
            ("f2", i + 0), ("f1", i + 1), ("ra", i + -2), ("rb", i + -2), ("up0", i + -1), ("up1", i + -1), ("down", i + -1), ("f3", i + 0), ("f4", i + 0), ("r1", i + -2), ("r0", i + -3),
        ):
            if 0 <= k < E:
                steps[name](k)

    out_ref[0] = part[me]
    for k in range(1, E):
        arrived(rb0.at[k], r0_recv.at[k])
        out_ref[k] = rb0[k]
    for copy in sends:
        copy.wait_send()


def body(tokens, expert_ids, affinity, w_gate, w_up, w_down):
    n = lax.axis_size("ep")
    experts = n // SPLIT
    rows, width = tokens.shape
    hid = w_gate.shape[2]
    dma = pltpu.SemaphoreType.DMA
    bf16 = jnp.bfloat16
    unit = (rows, width)
    hbm = pl.BlockSpec(memory_space=pltpu.MemorySpace.HBM)
    vmem = pl.BlockSpec(memory_space=pltpu.MemorySpace.VMEM)
    sums = pl.pallas_call(
        functools.partial(kernel, experts),
        out_shape=jax.ShapeDtypeStruct((experts,) + unit, bf16),
        in_specs=[hbm, hbm, hbm, hbm],
        out_specs=vmem,
        scratch_shapes=[
            pltpu.VMEM((n,) + unit, bf16),
            pltpu.VMEM((n,) + unit, bf16),
            pltpu.VMEM((experts, QUADS) + unit, bf16),
            pltpu.VMEM((experts, 2) + unit, bf16),
            pltpu.VMEM((experts,) + unit, bf16),
            pltpu.VMEM((experts,) + unit, bf16),
            pltpu.VMEM((width, hid), bf16),
            pltpu.VMEM((width, hid), bf16),
            pltpu.VMEM((hid, width), bf16),
            dma,
            dma((3,)),
            dma((n,)),
            dma((experts,)),
            dma((experts,)),
            dma((experts, 2)),
            dma((experts, QUADS)),
            dma((experts, QUADS)),
            dma((experts, QUADS)),
            dma((experts, 2)),
            dma((experts, 2)),
            dma((experts,)),
            dma((experts,)),
            dma((experts,)),
            dma((experts,)),
        ],
        compiler_params=pltpu.CompilerParams(
            collective_id=0, has_side_effects=True, vmem_limit_bytes=VMEM_LIMIT
        ),
    )(tokens, w_gate, w_up, w_down)
    routes = expert_ids.shape[1]
    share = route_scale * affinity / jnp.sum(affinity, axis=1, keepdims=True)
    z = lax.axis_index("ep") // SPLIT
    total = jnp.zeros(unit, jnp.float32)
    for k, step in enumerate(shifts(experts)):
        expert = (z + experts - step) % experts
        weight = sum(
            jnp.where(expert_ids[:, r] == expert, share[:, r], 0.0) for r in range(routes)
        )
        total = total + weight[:, None] * sums[k].astype(jnp.float32)
    return total.astype(bf16)


def solution(mesh):
    return jax.shard_map(
        body,
        mesh=mesh,
        in_specs=(
            P(("groups", "ep"), None),
            P(("groups", "ep"), None),
            P(("groups", "ep"), None),
            P("ep", None, None),
            P("ep", None, None),
            P("ep", None, None),
        ),
        out_specs=P(("groups", "ep"), None),
        check_vma=False,
    )
```

```python
import functools

import jax
import jax.numpy as jnp
from jax import lax
from jax.experimental import pallas as pl
from jax.experimental.pallas import tpu as pltpu
from jax.sharding import PartitionSpec as P

SPLIT = 8
CORES = 2
QUADS = SPLIT // CORES
MESH = pl.DeviceIdType.MESH
VMEM_LIMIT = 63 * 1024 * 1024

route_scale = 2.5


def tile_of(size, most):
    best = 128
    for tile in range(128, most + 1, 128):
        if size % tile == 0:
            best = tile
    return best


def shifts(experts):
    shift = [0]
    for step in range(1, experts // 2 + 1):
        shift += [step] if 2 * step == experts else [step, experts - step]
    return shift


def kernel(
    experts,
    tok_hbm, gate_hbm, up_hbm, down_hbm,
    out_ref,
    tok, part, rb3, rb2, rb1, rb0, gate_w, up_w, down_w,
    load_sem, w_sem, tok_recv, z_send, s1_send, s2_send, s3_send,
    r3_recv, r3_send, r2_recv, r2_send, r1_recv, r1_send, r0_recv, r0_send,
):
    E = experts
    rows, width = tok_hbm.shape
    hid = gate_w.shape[1]
    me = lax.axis_index("ep")
    z = me // SPLIT
    j = me % SPLIT
    c = j % 2
    x = (j // 2) % 2
    y = j // 4
    dx = 2 * (1 - 2 * x)
    dy = 4 * (1 - 2 * y)
    ja = j + (1 - c) * dy + c * dx
    jb = j + c * dy + (1 - c) * dx
    jab = j + dx + dy
    js = j + 1 - 2 * c
    base = z * SPLIT
    dev_a, dev_b, dev_s = base + ja, base + jb, base + js

    shift = shifts(E)

    def plane(k):
        return (z + shift[k]) % E

    def plane_back(k):
        return (z + E - shift[k]) % E

    loads = [
        pltpu.make_async_copy(tok_hbm, tok.at[me], load_sem),
        pltpu.make_async_copy(gate_hbm.at[0], gate_w, w_sem.at[0]),
        pltpu.make_async_copy(up_hbm.at[0], up_w, w_sem.at[1]),
        pltpu.make_async_copy(down_hbm.at[0], down_w, w_sem.at[2]),
    ]
    for load in loads:
        load.start()

    barrier = pltpu.get_barrier_semaphore()
    peers = [dev_a, dev_b, dev_s] + [((z + k) % E) * SPLIT + j for k in range(1, E)]
    for peer in peers:
        pl.semaphore_signal(barrier, inc=1, device_id={"ep": peer}, device_id_type=MESH)
    pl.semaphore_wait(barrier, len(peers))

    sends = []

    def send(src, dst, send_sem, recv_sem, device):
        copy = pltpu.make_async_remote_copy(
            src_ref=src, dst_ref=dst, send_sem=send_sem, recv_sem=recv_sem,
            device_id={"ep": device}, device_id_type=MESH,
        )
        copy.start()
        sends.append(copy)

    def arrived(dst, recv_sem):
        pltpu.make_async_remote_copy(
            src_ref=dst, dst_ref=dst, send_sem=load_sem, recv_sem=recv_sem,
            device_id={"ep": dev_s}, device_id_type=MESH,
        ).wait_recv()

    def tok_arrived(unit):
        arrived(tok.at[unit], tok_recv.at[unit])

    def pass_on(src, unit, sem, device):
        send(src, tok.at[unit], sem, tok_recv.at[unit], device)

    def own(k):
        return tok_hbm if k == 0 else tok.at[plane(k) * SPLIT + j]

    def f1(k):
        unit = plane(k) * SPLIT + j
        if k > 0:
            tok_arrived(unit)
        pass_on(own(k), unit, s1_send.at[k], dev_a)
        pass_on(own(k), unit, s2_send.at[k, 0], dev_b)
        pass_on(own(k), unit, s3_send.at[k, 0], dev_s)

    def f2(k):
        unit_a = plane(k) * SPLIT + ja
        tok_arrived(unit_a)
        pass_on(tok.at[unit_a], unit_a, s2_send.at[k, 1], dev_b)
        pass_on(tok.at[unit_a], unit_a, s3_send.at[k, 1], dev_s)

    def f3(k, at=2, jj=jb):
        unit = plane(k) * SPLIT + jj
        tok_arrived(unit)
        pass_on(tok.at[unit], unit, s3_send.at[k, at], dev_s)

    def f4(k):
        f3(k, 3, jab)

    k_tile = tile_of(width, 1792)
    n_tile = tile_of(width, 1024)

    held = {}

    def up(k, half):
        first = plane(k) * SPLIT
        if k == 0 and half == 0:
            for load in loads:
                load.wait()
        if half == 0:
            for q in range(QUADS):
                tok_arrived(first + 2 * q + (1 - c))

        def up_step(t, acc):
            cols = pl.ds(pl.multiple_of(t * k_tile, k_tile), k_tile)
            xs = tok[pl.ds(first, SPLIT), :, cols]
            xs = xs.astype(jnp.float32).reshape(SPLIT * rows, k_tile).astype(jnp.bfloat16)
            g, u = acc
            g = g + jnp.dot(xs, gate_w[cols, :], preferred_element_type=jnp.float32)
            u = u + jnp.dot(xs, up_w[cols, :], preferred_element_type=jnp.float32)
            return g, u

        zero = jnp.zeros((SPLIT * rows, hid), jnp.float32)
        count = width // k_tile
        if half == 0:
            held[k] = lax.fori_loop(0, count // 2, up_step, (zero, zero))
        else:
            g, u = lax.fori_loop(count // 2, count, up_step, held[k])
            held[k] = (jax.nn.silu(g) * u).astype(jnp.bfloat16)

    def down(k):
        first = plane(k) * SPLIT
        hidden = held.pop(k)

        def down_step(t, carry):
            cols = pl.ds(pl.multiple_of(t * n_tile, n_tile), n_tile)
            d = jnp.dot(hidden, down_w[:, cols], preferred_element_type=jnp.float32)
            part[pl.ds(first, SPLIT), :, cols] = d.reshape(SPLIT, rows, n_tile).astype(jnp.bfloat16)
            return carry

        lax.fori_loop(0, width // n_tile, down_step, 0)
        for q in range(QUADS):
            send(part.at[first + 2 * q + (1 - c)], rb3.at[k, q],
                 r3_send.at[k, q], r3_recv.at[k, q], dev_s)

    f32 = jnp.float32

    def ra(k, at=1, jj=jab):
        unit, q = plane(k) * SPLIT + jj, jj // 2
        arrived(rb3.at[k, q], r3_recv.at[k, q])
        part[unit] = (part[unit].astype(f32) + rb3[k, q].astype(f32)).astype(jnp.bfloat16)
        send(part.at[unit], rb2.at[k, at], r2_send.at[k, at], r2_recv.at[k, at], dev_b)

    def rb(k):
        ra(k, 0, jb)

    def r1(k):
        unit, q = plane(k) * SPLIT + ja, ja // 2
        arrived(rb3.at[k, q], r3_recv.at[k, q])
        arrived(rb2.at[k, 1], r2_recv.at[k, 1])
        part[unit] = (
            part[unit].astype(f32) + rb3[k, q].astype(f32) + rb2[k, 1].astype(f32)
        ).astype(jnp.bfloat16)
        send(part.at[unit], rb1.at[k], r1_send.at[k], r1_recv.at[k], dev_a)

    def r0(k):
        unit, q = plane(k) * SPLIT + j, j // 2
        arrived(rb3.at[k, q], r3_recv.at[k, q])
        arrived(rb2.at[k, 0], r2_recv.at[k, 0])
        arrived(rb1.at[k], r1_recv.at[k])
        part[unit] = (
            (part[unit].astype(f32) + rb3[k, q].astype(f32))
            + (rb2[k, 0].astype(f32) + rb1[k].astype(f32))
        ).astype(jnp.bfloat16)
        if k > 0:
            send(part.at[unit], rb0.at[k], r0_send.at[k], r0_recv.at[k], unit)

    for k in range(1, E):
        pass_on(tok_hbm, me, z_send.at[k], plane_back(k) * SPLIT + j)
    steps = {
        "f1": f1, "f2": f2, "f3": f3, "f4": f4,
        "up0": lambda k: up(k, 0), "up1": lambda k: up(k, 1), "down": down,
        "ra": ra, "rb": rb, "r1": r1, "r0": r0,
    }
    for i in range(-1, E + 5):
        for name, k in (
            ("f2", i + 0), ("f1", i + 1), ("ra", i + -2), ("rb", i + -2), ("up0", i + -1), ("up1", i + -1), ("down", i + -1), ("f3", i + 0), ("f4", i + 0), ("r1", i + -2), ("r0", i + -3),
        ):
            if 0 <= k < E:
                steps[name](k)

    out_ref[0] = part[me]
    for k in range(1, E):
        arrived(rb0.at[k], r0_recv.at[k])
        out_ref[k] = rb0[k]
    for copy in sends:
        copy.wait_send()


def body(tokens, expert_ids, affinity, w_gate, w_up, w_down):
    n = lax.axis_size("ep")
    experts = n // SPLIT
    rows, width = tokens.shape
    hid = w_gate.shape[2]
    dma = pltpu.SemaphoreType.DMA
    bf16 = jnp.bfloat16
    unit = (rows, width)
    hbm = pl.BlockSpec(memory_space=pltpu.MemorySpace.HBM)
    vmem = pl.BlockSpec(memory_space=pltpu.MemorySpace.VMEM)
    sums = pl.pallas_call(
        functools.partial(kernel, experts),
        out_shape=jax.ShapeDtypeStruct((experts,) + unit, bf16),
        in_specs=[hbm, hbm, hbm, hbm],
        out_specs=vmem,
        scratch_shapes=[
            pltpu.VMEM((n,) + unit, bf16),
            pltpu.VMEM((n,) + unit, bf16),
            pltpu.VMEM((experts, QUADS) + unit, bf16),
            pltpu.VMEM((experts, 2) + unit, bf16),
            pltpu.VMEM((experts,) + unit, bf16),
            pltpu.VMEM((experts,) + unit, bf16),
            pltpu.VMEM((width, hid), bf16),
            pltpu.VMEM((width, hid), bf16),
            pltpu.VMEM((hid, width), bf16),
            dma,
            dma((3,)),
            dma((n,)),
            dma((experts,)),
            dma((experts,)),
            dma((experts, 2)),
            dma((experts, QUADS)),
            dma((experts, QUADS)),
            dma((experts, QUADS)),
            dma((experts, 2)),
            dma((experts, 2)),
            dma((experts,)),
            dma((experts,)),
            dma((experts,)),
            dma((experts,)),
        ],
        compiler_params=pltpu.CompilerParams(
            collective_id=0, has_side_effects=True, vmem_limit_bytes=VMEM_LIMIT
        ),
    )(tokens, w_gate, w_up, w_down)
    routes = expert_ids.shape[1]
    z = lax.axis_index("ep") // SPLIT
    total_affinity = sum(affinity[:, r : r + 1] for r in range(routes))
    expert = (z + experts - jnp.array(shifts(experts), jnp.int32)[None, :]) % experts
    weight = sum(
        jnp.where(
            expert_ids[:, r : r + 1] == expert,
            route_scale * affinity[:, r : r + 1] / total_affinity,
            0.0,
        )
        for r in range(routes)
    )
    total = sum(weight[:, k : k + 1] * sums[k].astype(jnp.float32) for k in range(experts))
    return total.astype(bf16)


def solution(mesh):
    return jax.shard_map(
        body,
        mesh=mesh,
        in_specs=(
            P(("groups", "ep"), None),
            P(("groups", "ep"), None),
            P(("groups", "ep"), None),
            P("ep", None, None),
            P("ep", None, None),
            P("ep", None, None),
        ),
        out_specs=P(("groups", "ep"), None),
        check_vma=False,
    )
```
